32 devices in a mesh: dp: 16 (over z, y, x), tensor: 2 (over core).
Axes of the slice: x: 2, y: 2, z: 4, core: 2. Of those that a mesh axis runs over, the one named last changes fastest.
Arguments:
- tokens: bfloat16 [4096, 2048], P(('dp', 'tensor')), may hold values from -6 to 6
- routes: int32 [4096, 8], P('dp'), may hold values from 0 to 15, all different within a row; in each aligned block of 256 rows (0 to 255, 256 to 511, ...) at most 160 rows name the same one
- attention_gain: bfloat16 [2048], replicated, may hold values from 0.5 to 1.5
- query_weight: bfloat16 [2048, 2048], P('dp', 'tensor'), may hold values from -0.125 to 0.125
- key_weight: bfloat16 [2048, 2048], P('dp', 'tensor'), may hold values from -0.125 to 0.125
- value_weight: bfloat16 [2048, 2048], P('dp', 'tensor'), may hold values from -0.125 to 0.125
- query_gain: bfloat16 [2048], replicated, may hold values from 0.5 to 1.5
- key_gain: bfloat16 [2048], replicated, may hold values from 0.5 to 1.5
- output_weight: bfloat16 [2048, 2048], P('tensor', 'dp'), may hold values from -1 to 1
- feedforward_gain: bfloat16 [2048], replicated, may hold values from 0.5 to 1.5
- router_weight: bfloat16 [2048, 16], replicated, may hold values from -0.125 to 0.125
- gate_weight: bfloat16 [16, 2048, 1024], P('dp', None, 'tensor'), may hold values from -0.125 to 0.125
- up_weight: bfloat16 [16, 2048, 1024], P('dp', None, 'tensor'), may hold values from -0.125 to 0.125
- down_weight: bfloat16 [16, 1024, 2048], P('dp', 'tensor'), may hold values from -1.5 to 1.5
- grad_out: bfloat16 [4096, 2048], P(('dp', 'tensor')), may hold values from -6 to 6
Outputs:
- block_out: bfloat16 [4096, 2048], P(('dp', 'tensor'))
- grad_tokens: bfloat16 [4096, 2048], P(('dp', 'tensor'))
- grad_attention_gain: float32 [2048], replicated
- grad_query_weight: float32 [2048, 2048], P('dp', 'tensor')
- grad_key_weight: float32 [2048, 2048], P('dp', 'tensor')
- grad_value_weight: float32 [2048, 2048], P('dp', 'tensor')
- grad_query_gain: float32 [2048], replicated
- grad_key_gain: float32 [2048], replicated
- grad_output_weight: float32 [2048, 2048], P('tensor', 'dp')
- grad_feedforward_gain: float32 [2048], replicated
- grad_router_weight: float32 [2048, 16], replicated
- grad_gate_weight: float32 [16, 2048, 1024], P('dp', None, 'tensor')
- grad_up_weight: float32 [16, 2048, 1024], P('dp', None, 'tensor')
- grad_down_weight: float32 [16, 1024, 2048], P('dp', 'tensor')
The draws below stay inside these ranges and needn't reach their ends.
Inputs may be any that keep to these rules, and one draw needn't show every extreme that they name: `routes`: each row names 8 different experts; in each aligned block of 256 rows (one sequence) no expert is named by more than 160 rows, a bound that some block reaches.
All inputs are finite; a program needn't handle non-finite values.
Results may differ from the reference program's by a relative error of at most 0.019.
Values may be sent and summed in bfloat16 or wider, within the bound.
No kernel may reach another device: no remote copies, remote signals or barrier semaphores. Data moves between devices by JAX's collectives and lax.ppermute only.
A program may use at most 320 MiB of HBM per device.

```python
import math
import jax
import jax.numpy as jnp
import numpy as np
from jax import lax

D = 2048
HEADS = 16
HD = 128
FF = 1024
TOP = 8
SEQ = 256
EXPERTS = 16
QD = 2048
TOKENS = 4096
CAP = 160
N_DP = 16


def levels(rng, shape, split, low, largest):
    level = 1.0
    for dim, blocks in split:
        steps = jax.random.uniform(jax.random.fold_in(jax.random.fold_in(rng, 6), dim), (blocks,), jnp.float32, low / len(split), largest / len(split))
        level = level * jnp.repeat(jnp.exp(steps), shape[dim] // blocks).reshape((-1,) + (1,) * (len(shape) - 1 - dim))
    return level


def routed_block(stream_key, own, number, rows, amount, top, most, skew):
    ranking = jax.random.permutation(stream_key, amount)
    crowded, ordinary = load_shares(amount, rows * top, most, skew, True), load_shares(amount, rows * top, most, skew, False)
    places = jnp.arange(amount)

    def named(tallies, offset_by):
        used = int((tallies > 0).sum())
        fixed = max(1, used // 4)
        passed = fixed + (places - fixed + offset_by * (used - fixed)) % max(1, amount - fixed)
        return jnp.zeros((amount,), jnp.int32).at[ranking[jnp.where(places < fixed, places, passed)]].set(jnp.asarray(tallies, jnp.int32))

    tallies = jnp.where(number % 4 == 0, named(crowded, number // 4), named(ordinary, number - number // 4 - 1))
    mixed = jax.random.permutation(jax.random.fold_in(own, 3), amount)
    donor, taker = mixed[0:amount // 2 * 2:2], mixed[1:amount // 2 * 2:2]
    margin = jnp.minimum(tallies[donor] - 1, most - tallies[taker]) // 2
    margin = jnp.where((donor == ranking[0]) | (taker == ranking[0]) | (tallies[taker] == 0), 0, jnp.maximum(margin, 0))
    passed = jax.random.randint(jax.random.fold_in(own, 4), (amount // 2,), 0, 1 << 20) % (margin + 1)
    tallies = tallies.at[donor].add(-passed).at[taker].add(passed)
    labels = jnp.searchsorted(jnp.cumsum(tallies), jnp.arange(rows * top), side="right").astype(jnp.int32)
    table = labels.reshape(top, rows).T
    table = table[jax.random.permutation(jax.random.fold_in(own, 1), rows)]
    offset_by = jax.random.randint(jax.random.fold_in(own, 2), (rows, 1), 0, top)
    return jnp.take_along_axis(table, (jnp.arange(top)[None, :] + offset_by) % top, axis=1)


def load_shares(count, total, reach, skew, full):
    weights = [(1 << 20) // math.isqrt(grade ** skew) + 1 for grade in range(1, count + 1)]
    largest = reach if full else min(reach, max(-(-total // count), total * weights[0] // sum(weights)))
    least = 1 if total - largest >= count - 1 else 0
    given, spare = [largest] + [least] * (count - 1), total - largest - least * (count - 1)
    while spare > 0:
        movable = [i for i in range(1, count) if given[i] < largest] or [i for i in range(1, count) if given[i] < reach]
        pool, budget = sum([weights[i] for i in movable]), spare
        for i in movable:
            more = min(reach - given[i], max(1, budget * weights[i] // pool), spare)
            given[i] = given[i] + more
            spare = spare - more
    return np.array(given)


def gaussian(own_key, dims, spread, bound, shards=(), held_as=jnp.bfloat16):
    factor_of = levels(own_key, dims, shards, -0.22, 0.18) if shards else 1.0
    values = jax.random.normal(own_key, dims, jnp.float32) * spread * factor_of
    return jnp.minimum(jnp.maximum(values, -bound), bound).astype(held_as)


def setup_inputs(seed: int = 0) -> dict:
    key_list = jax.random.split(jax.random.key(seed), 16)
    tokens = gaussian(key_list[0], (TOKENS, D), 1.0, 6.0, ((0, 32),))
    routes_keys = jax.random.split(jax.random.fold_in(key_list[1], 1), TOKENS // SEQ)
    routes_turns = jax.random.permutation(jax.random.fold_in(key_list[1], 3), TOKENS // SEQ)
    routes = jax.vmap(lambda own, number: routed_block(jax.random.fold_in(key_list[1], 2), own, number, SEQ, EXPERTS, TOP, CAP, 1))(routes_keys, routes_turns).reshape((TOKENS, TOP))
    attention_gain = jnp.clip(1.0 + 0.1 * jax.random.normal(key_list[2], (D,), jnp.float32), 0.5, 1.5).astype(jnp.bfloat16)
    query_weight = gaussian(key_list[3], (D, QD), D ** -0.5, 0.125, ((0, 16), (1, 2)))
    key_weight = gaussian(key_list[4], (D, QD), D ** -0.5, 0.125, ((0, 16), (1, 2)))
    value_weight = gaussian(key_list[5], (D, QD), D ** -0.5, 0.125, ((0, 16), (1, 2)))
    query_gain = jnp.clip(1.0 + 0.1 * jax.random.normal(key_list[6], (QD,), jnp.float32), 0.5, 1.5).astype(jnp.bfloat16)
    key_gain = jnp.clip(1.0 + 0.1 * jax.random.normal(key_list[7], (QD,), jnp.float32), 0.5, 1.5).astype(jnp.bfloat16)
    output_weight = gaussian(key_list[8], (QD, D), (HD // 4) ** -0.5, 1.0, ((0, 2), (1, 16)))
    feedforward_gain = jnp.clip(1.0 + 0.1 * jax.random.normal(key_list[9], (D,), jnp.float32), 0.5, 1.5).astype(jnp.bfloat16)
    router_weight = gaussian(key_list[10], (D, EXPERTS), D ** -0.5, 0.125)
    gate_weight = gaussian(key_list[11], (EXPERTS, D, FF), D ** -0.5, 0.125, ((0, 16), (2, 2)))
    up_weight = gaussian(key_list[12], (EXPERTS, D, FF), D ** -0.5, 0.125, ((0, 16), (2, 2)))
    down_weight = gaussian(key_list[13], (EXPERTS, FF, D), (max(FF // 64, 1)) ** -0.5, 1.5, ((0, 16), (1, 2)))
    grad_out = gaussian(key_list[14], (TOKENS, D), 1.0, 6.0, ((0, 32),))
    return dict(tokens=tokens, routes=routes, attention_gain=attention_gain, query_weight=query_weight, key_weight=key_weight, value_weight=value_weight, query_gain=query_gain, key_gain=key_gain, output_weight=output_weight, feedforward_gain=feedforward_gain, router_weight=router_weight, gate_weight=gate_weight, up_weight=up_weight, down_weight=down_weight, grad_out=grad_out)


EPS = 1e-05

def row_scale(values):
    return lax.rsqrt(lax.optimization_barrier(jnp.mean(values * values, axis=-1, keepdims=True)) + EPS)

def rotate_half(values):
    middle = values.shape[-1] // 2
    return jnp.concatenate([-values[..., middle:], values[..., :middle]], axis=-1)

def rope_tables(length, head_dim):
    position = jnp.arange(length).astype(jnp.float32)
    inverse = 1.0 / 10000.0 ** (jnp.arange(0, head_dim, 2).astype(jnp.float32) / head_dim)
    angles = position[:, None] * inverse[None, :]
    angles = jnp.concatenate([angles, angles], axis=-1)
    return (jnp.cos(angles)[:, None, :], jnp.sin(angles)[:, None, :])

def slot_positions(routes, experts):
    flat_route = routes.reshape(-1)
    onehot = (flat_route[:, None] == jnp.arange(experts).astype(jnp.int32)[None, :]).astype(jnp.int32)
    before = jnp.cumsum(onehot, axis=0) - onehot
    return (flat_route, lax.optimization_barrier(jnp.sum(before * onehot, axis=1)))

def norm_backward(upstream, source, scale, gain):
    product = upstream * gain
    return scale * product - source * scale * scale * scale * lax.optimization_barrier(jnp.mean(product * source, axis=-1, keepdims=True))

def matmul(left, right):
    return jnp.dot(left, right, preferred_element_type=jnp.float32)

def sequence_pass(tokens, grad_out, routes, weights):
    attention_gain, query_weight, key_weight, value_weight, query_gain, key_gain, output_weight, feedforward_gain, router_weight, gate_full, up_full, down_full = weights
    length = tokens.shape[0]
    tok_f = tokens.astype(jnp.float32)
    attn_gf = attention_gain.astype(jnp.float32)
    ff_gf = feedforward_gain.astype(jnp.float32)
    query_gf = query_gain.astype(jnp.float32)
    key_gf = key_gain.astype(jnp.float32)
    scale_one = row_scale(tok_f)
    normed_one = (tok_f * scale_one * attn_gf).astype(jnp.bfloat16)
    query_proj = matmul(normed_one, query_weight)
    key_proj = matmul(normed_one, key_weight)
    value_proj = matmul(normed_one, value_weight).astype(jnp.bfloat16)
    query_scale = row_scale(query_proj)
    key_scale = row_scale(key_proj)
    query_norm = query_proj * query_scale * query_gf
    key_norm = key_proj * key_scale * key_gf
    cosine, sine = rope_tables(length, HD)
    query_heads = query_norm.reshape(length, HEADS, HD)
    key_heads = key_norm.reshape(length, HEADS, HD)
    query_rot = (query_heads * cosine + rotate_half(query_heads) * sine).astype(jnp.bfloat16)
    key_rot = (key_heads * cosine + rotate_half(key_heads) * sine).astype(jnp.bfloat16)
    value_heads = value_proj.reshape(length, HEADS, HD)
    causal = jnp.arange(length)[:, None] >= jnp.arange(length)[None, :]
    inv_root = 1.0 / math.sqrt(HD)
    scores = jnp.einsum('qhd,khd->hqk', query_rot.astype(jnp.float32), key_rot.astype(jnp.float32)) * inv_root
    scores = jnp.where(causal[None], scores, -jnp.inf)
    top_score = lax.optimization_barrier(jnp.max(scores, axis=-1, keepdims=True))
    log_total = top_score + jnp.log(lax.optimization_barrier(jnp.sum(jnp.exp(scores - top_score), axis=-1, keepdims=True)))
    attn_prob = jnp.exp(scores - log_total)
    prob_bf = attn_prob.astype(jnp.bfloat16)
    context = jnp.einsum('hqk,khd->qhd', prob_bf.astype(jnp.float32), value_heads.astype(jnp.float32))
    context = context.reshape(length, HEADS * HD).astype(jnp.bfloat16)
    resid = tok_f + matmul(context, output_weight)
    scale_two = row_scale(resid)
    normed_two = (resid * scale_two * ff_gf).astype(jnp.bfloat16)
    logits = matmul(normed_two, router_weight)
    probs = jax.nn.softmax(logits, axis=-1)
    combine = jnp.take_along_axis(probs, routes, axis=1)
    flat_route, slots = slot_positions(routes, EXPERTS)
    pair_token = jnp.arange(length * TOP) // TOP
    dispatch = jnp.zeros((EXPERTS, CAP, D), jnp.bfloat16).at[flat_route, slots].set(normed_two[pair_token])
    dispatch_f = dispatch.astype(jnp.float32)
    gate_act = jnp.einsum('ecd,edf->ecf', dispatch_f, gate_full)
    up_act = jnp.einsum('ecd,edf->ecf', dispatch_f, up_full)
    sigma = jax.nn.sigmoid(gate_act)
    hidden = (gate_act * sigma * up_act).astype(jnp.bfloat16)
    hidden_f = hidden.astype(jnp.float32)
    expert_out = jnp.einsum('ecf,efd->ecd', hidden_f, down_full)
    picked = expert_out[flat_route, slots].reshape(length, TOP, D)
    moe = lax.optimization_barrier(jnp.sum(combine[:, :, None] * picked, axis=1))
    block_out = (resid + moe).astype(jnp.bfloat16)
    dout_f = grad_out.astype(jnp.float32)
    pair_rows = combine.reshape(-1)[:, None] * dout_f[pair_token]
    grad_expert = jnp.zeros((EXPERTS, CAP, D), jnp.float32).at[flat_route, slots].set(pair_rows).astype(jnp.bfloat16)
    grad_combine = lax.optimization_barrier(jnp.sum(dout_f[:, None, :] * picked, axis=-1))
    grad_expert_f = grad_expert.astype(jnp.float32)
    grad_hidden = jnp.einsum('ecd,efd->ecf', grad_expert_f, down_full)
    grad_down = jnp.einsum('ecf,ecd->efd', hidden_f, grad_expert_f)
    grad_gate = (grad_hidden * up_act * sigma * (1.0 + gate_act * (1.0 - sigma))).astype(jnp.bfloat16).astype(jnp.float32)
    grad_up = (grad_hidden * gate_act * sigma).astype(jnp.bfloat16).astype(jnp.float32)
    grad_gate_w = jnp.einsum('ecd,ecf->edf', dispatch_f, grad_gate)
    grad_up_w = jnp.einsum('ecd,ecf->edf', dispatch_f, grad_up)
    grad_dispatch = (jnp.einsum('ecf,edf->ecd', grad_gate, gate_full) + jnp.einsum('ecf,edf->ecd', grad_up, up_full)).astype(jnp.bfloat16)
    back_rows = grad_dispatch.astype(jnp.float32)[flat_route, slots].reshape(length, TOP, D)
    onehot_routes = (routes[:, :, None] == jnp.arange(EXPERTS).astype(jnp.int32)[None, None, :]).astype(jnp.float32)
    grad_prob = lax.optimization_barrier(jnp.sum(grad_combine[:, :, None] * onehot_routes, axis=1))
    grad_logit = probs * (grad_prob - lax.optimization_barrier(jnp.sum(probs * grad_prob, axis=-1, keepdims=True)))
    router_f = router_weight.astype(jnp.float32)
    grad_two = lax.optimization_barrier(jnp.sum(back_rows, axis=1)) + jnp.dot(grad_logit, router_f.T, precision=lax.Precision.HIGHEST)
    grad_router = jnp.dot(normed_two.astype(jnp.float32).T, grad_logit, precision=lax.Precision.HIGHEST)
    grad_ffgain = lax.optimization_barrier(jnp.sum(grad_two * resid * scale_two, axis=0))
    grad_resid = dout_f + norm_backward(grad_two, resid, scale_two, ff_gf)
    grad_attn = grad_resid.astype(jnp.bfloat16)
    grad_out_w = matmul(context.T, grad_attn)
    grad_context = matmul(grad_attn, output_weight.T).astype(jnp.bfloat16).reshape(length, HEADS, HD)
    grad_context_f = grad_context.astype(jnp.float32)
    grad_value_f = jnp.einsum('hqk,qhd->khd', prob_bf.astype(jnp.float32), grad_context_f)
    grad_prob_att = jnp.einsum('qhd,khd->hqk', grad_context_f, value_heads.astype(jnp.float32))
    delta = lax.optimization_barrier(jnp.sum(attn_prob * grad_prob_att, axis=-1, keepdims=True))
    grad_scores = (attn_prob * (grad_prob_att - delta) * inv_root).astype(jnp.bfloat16).astype(jnp.float32)
    grad_query_rot = jnp.einsum('hqk,khd->qhd', grad_scores, key_rot.astype(jnp.float32))
    grad_key_rot = jnp.einsum('hqk,qhd->khd', grad_scores, query_rot.astype(jnp.float32))
    grad_query_norm = (grad_query_rot * cosine - rotate_half(grad_query_rot * sine)).reshape(length, HEADS * HD)
    grad_key_norm = (grad_key_rot * cosine - rotate_half(grad_key_rot * sine)).reshape(length, HEADS * HD)
    grad_qgain = lax.optimization_barrier(jnp.sum(grad_query_norm * query_proj * query_scale, axis=0))
    grad_kgain = lax.optimization_barrier(jnp.sum(grad_key_norm * key_proj * key_scale, axis=0))
    grad_query = norm_backward(grad_query_norm, query_proj, query_scale, query_gf).astype(jnp.bfloat16)
    grad_key = norm_backward(grad_key_norm, key_proj, key_scale, key_gf).astype(jnp.bfloat16)
    grad_value = grad_value_f.reshape(length, HEADS * HD).astype(jnp.bfloat16)
    grad_query_w = matmul(normed_one.T, grad_query)
    grad_key_w = matmul(normed_one.T, grad_key)
    grad_value_w = matmul(normed_one.T, grad_value)
    grad_one = matmul(grad_query, query_weight.T) + matmul(grad_key, key_weight.T) + matmul(grad_value, value_weight.T)
    grad_again = lax.optimization_barrier(jnp.sum(grad_one * tok_f * scale_one, axis=0))
    grad_tokens = (grad_resid + norm_backward(grad_one, tok_f, scale_one, attn_gf)).astype(jnp.bfloat16)
    grads = (grad_again, grad_query_w, grad_key_w, grad_value_w, grad_qgain, grad_kgain, grad_out_w, grad_ffgain, grad_router, grad_gate_w, grad_up_w, grad_down)
    return (block_out, grad_tokens, grads)

def reference(tokens, routes, attention_gain, query_weight, key_weight, value_weight, query_gain, key_gain, output_weight, feedforward_gain, router_weight, gate_weight, up_weight, down_weight, grad_out):
    weights = (attention_gain, query_weight, key_weight, value_weight, query_gain, key_gain, output_weight, feedforward_gain, router_weight, gate_weight.astype(jnp.float32), up_weight.astype(jnp.float32), down_weight.astype(jnp.float32))
    zeros = (jnp.zeros((D,), jnp.float32), jnp.zeros((D, QD), jnp.float32), jnp.zeros((D, QD), jnp.float32), jnp.zeros((D, QD), jnp.float32), jnp.zeros((QD,), jnp.float32), jnp.zeros((QD,), jnp.float32), jnp.zeros((QD, D), jnp.float32), jnp.zeros((D,), jnp.float32), jnp.zeros((D, EXPERTS), jnp.float32), jnp.zeros((EXPERTS, D, FF), jnp.float32), jnp.zeros((EXPERTS, D, FF), jnp.float32), jnp.zeros((EXPERTS, FF, D), jnp.float32))

    def advance(totals, item):
        piece, grad_piece, route_piece = item
        block_piece, grad_tok_piece, grads = sequence_pass(piece, grad_piece, route_piece, weights)
        totals = jax.tree.map(lambda left, right: left + right, totals, grads)
        return (totals, (block_piece, grad_tok_piece))
    totals, (block_all, grad_tok_all) = lax.scan(advance, zeros, (tokens.reshape(N_DP, SEQ, D), grad_out.reshape(N_DP, SEQ, D), routes.reshape(N_DP, SEQ, TOP)))
    return (block_all.reshape(TOKENS, D), grad_tok_all.reshape(TOKENS, D), totals[0], totals[1], totals[2], totals[3], totals[4], totals[5], totals[6], totals[7], totals[8], totals[9], totals[10], totals[11])
```

```python
import functools
import math

import jax
import jax.numpy as jnp
from jax import lax
from jax.experimental import pallas as pl
from jax.experimental.pallas import tpu as pltpu
from jax.sharding import PartitionSpec as P

HD = 128


EPS = 1e-05


def row_scale(values):
    return lax.rsqrt(jnp.mean(values * values, axis=-1, keepdims=True) + EPS)


def rotate_half(values):
    middle = values.shape[-1] // 2
    return jnp.concatenate([-values[..., middle:], values[..., :middle]], axis=-1)


def rope_tables(length, head_dim):
    position = jnp.arange(length).astype(jnp.float32)
    inverse = 1.0 / 10000.0 ** (jnp.arange(0, head_dim, 2).astype(jnp.float32) / head_dim)
    angles = position[:, None] * inverse[None, :]
    angles = jnp.concatenate([angles, angles], axis=-1)
    return (jnp.cos(angles)[:, None, :], jnp.sin(angles)[:, None, :])


def slot_positions(routes, experts):
    flat_route = routes.reshape(-1)
    onehot = (flat_route[:, None] == jnp.arange(experts)[None, :]).astype(jnp.int32)
    before = jnp.cumsum(onehot, axis=0) - onehot
    return (flat_route, jnp.sum(before * onehot, axis=1))


def norm_backward(upstream, source, scale, gain):
    product = upstream * gain
    return scale * product - source * scale * scale * scale * jnp.mean(
        product * source, axis=-1, keepdims=True
    )


def matmul(left, right):
    return jnp.dot(left, right, preferred_element_type=jnp.float32)


def matmul_right_t(left, right):
    return jnp.einsum("ta,ba->tb", left, right, preferred_element_type=jnp.float32)


def matmul_left_t(left, right):
    return jnp.einsum("ta,tb->ab", left, right, preferred_element_type=jnp.float32)


def gather_rows(values):
    return lax.all_gather(values, "tensor", axis=0, tiled=True)


def sum_rows(values):
    return lax.psum_scatter(values, "tensor", scatter_dimension=0, tiled=True)


def feature_totals(first, second):
    return lax.psum((first, second), "tensor")


def move_experts(values):
    return lax.all_to_all(values, "dp", split_axis=0, concat_axis=0, tiled=True)


def by_capacity(
    tokens,
    routes,
    attention_gain,
    query_weight,
    key_weight,
    value_weight,
    query_gain,
    key_gain,
    output_weight,
    feedforward_gain,
    router_weight,
    gate_weight,
    up_weight,
    down_weight,
    grad_out,
):
    rank = lax.axis_index("tensor")
    ways = lax.axis_size("tensor")
    groups = lax.axis_size("dp")
    local_experts = gate_weight.shape[0]
    experts = local_experts * groups
    width = tokens.shape[1]
    length = routes.shape[0]
    top = routes.shape[1]
    qd_local = query_weight.shape[1]
    heads_local = qd_local // HD
    qd_total = qd_local * ways
    capacity = max(2, length * top * 5 // (4 * experts * ways) * ways)
    half_cap = capacity // ways
    inv_root = 1.0 / math.sqrt(HD)
    tok_f = tokens.astype(jnp.float32)
    attn_gf = attention_gain.astype(jnp.float32)
    ff_gf = feedforward_gain.astype(jnp.float32)
    query_gloc = lax.dynamic_slice_in_dim(query_gain, rank * qd_local, qd_local).astype(jnp.float32)
    key_gloc = lax.dynamic_slice_in_dim(key_gain, rank * qd_local, qd_local).astype(jnp.float32)
    weights_full = (
        lax.all_gather(query_weight, "dp", axis=0, tiled=True),
        lax.all_gather(key_weight, "dp", axis=0, tiled=True),
        lax.all_gather(value_weight, "dp", axis=0, tiled=True),
        lax.all_gather(output_weight, "dp", axis=1, tiled=True),
    )
    query_full, key_full, value_full, output_full = weights_full
    scale_one = row_scale(tok_f)
    normed_one = gather_rows((tok_f * scale_one * attn_gf).astype(jnp.bfloat16))
    query_proj = matmul(normed_one, query_full)
    key_proj = matmul(normed_one, key_full)
    value_proj = matmul(normed_one, value_full).astype(jnp.bfloat16)
    query_total, key_total = feature_totals(
        jnp.sum(query_proj * query_proj, axis=-1, keepdims=True),
        jnp.sum(key_proj * key_proj, axis=-1, keepdims=True),
    )
    query_scale = lax.rsqrt(query_total / qd_total + EPS)
    key_scale = lax.rsqrt(key_total / qd_total + EPS)
    cosine, sine = rope_tables(length, HD)
    query_heads = (query_proj * query_scale * query_gloc).reshape(length, heads_local, HD)
    key_heads = (key_proj * key_scale * key_gloc).reshape(length, heads_local, HD)
    query_rot = (query_heads * cosine + rotate_half(query_heads) * sine).astype(jnp.bfloat16)
    key_rot = (key_heads * cosine + rotate_half(key_heads) * sine).astype(jnp.bfloat16)
    value_heads = value_proj.reshape(length, heads_local, HD)
    causal = jnp.arange(length)[:, None] >= jnp.arange(length)[None, :]

    def score_block(query_part, key_part):
        raw = (
            jnp.einsum("qhd,khd->hqk", query_part, key_part, preferred_element_type=jnp.float32)
            * inv_root
        )
        return jnp.where(causal[None], raw, -jnp.inf)

    scores = score_block(query_rot, key_rot)
    top_score = jnp.max(scores, axis=-1, keepdims=True)
    log_total = top_score + jnp.log(jnp.sum(jnp.exp(scores - top_score), axis=-1, keepdims=True))
    prob_bf = jnp.exp(scores - log_total).astype(jnp.bfloat16)
    context = jnp.einsum("hqk,khd->qhd", prob_bf, value_heads, preferred_element_type=jnp.float32)
    context = context.reshape(length, qd_local).astype(jnp.bfloat16)
    resid = tok_f + sum_rows(matmul(context, output_full))
    scale_two = row_scale(resid)
    normed_two = gather_rows((resid * scale_two * ff_gf).astype(jnp.bfloat16))
    probs = jax.nn.softmax(matmul(normed_two, router_weight), axis=-1)
    combine = jnp.take_along_axis(probs, routes, axis=1).reshape(-1)
    flat_route, slots = slot_positions(routes, experts)
    owner = (
        jnp.full((experts * capacity,), -1, jnp.int32)
        .at[flat_route * capacity + slots]
        .set(jnp.arange(length * top))
    )
    source_rows = jnp.take(normed_two, jnp.maximum(owner, 0) // top, axis=0)
    dispatch = jnp.where((owner >= 0)[:, None], source_rows, jnp.zeros((), jnp.bfloat16))
    dispatch = dispatch.reshape(experts, capacity, width)
    blocks = move_experts(dispatch).reshape(groups, local_experts, capacity, width)
    gate_act = jnp.einsum("sjcd,jdf->sjcf", blocks, gate_weight, preferred_element_type=jnp.float32)
    up_act = jnp.einsum("sjcd,jdf->sjcf", blocks, up_weight, preferred_element_type=jnp.float32)
    sigma = jax.nn.sigmoid(gate_act)
    hidden = (gate_act * sigma * up_act).astype(jnp.bfloat16)
    blocks, gate_act, up_act, sigma, hidden = (blocks, gate_act, up_act, sigma, hidden)
    partial_out = jnp.einsum(
        "sjcf,jfd->sjcd", hidden, down_weight, preferred_element_type=jnp.float32
    )
    partial_out = partial_out.reshape(experts, capacity, width)
    summed = lax.psum_scatter(
        partial_out.astype(jnp.bfloat16), "tensor", scatter_dimension=1, tiled=True
    ).astype(jnp.float32)
    returned = lax.all_to_all(
        summed.astype(jnp.bfloat16), "dp", split_axis=0, concat_axis=0, tiled=True
    ).astype(summed.dtype)
    first_slot = rank * half_cap
    offset = slots - first_slot
    inside = (offset >= 0) & (offset < half_cap)
    picked = jnp.take(
        returned.reshape(experts * half_cap, width),
        flat_route * half_cap + jnp.clip(offset, 0, half_cap - 1),
        axis=0,
    ).reshape(length, top, width)
    pair_weight = jnp.where(inside, combine, 0.0).reshape(length, top)
    moe = sum_rows(jnp.sum(pair_weight[:, :, None] * picked, axis=1))
    block_out = (resid + moe).astype(jnp.bfloat16)
    dout_all = gather_rows(grad_out)
    dout_f = dout_all.astype(jnp.float32)
    grad_combine = jnp.where(
        inside.reshape(length, top), jnp.sum(dout_f[:, None, :] * picked, axis=-1), 0.0
    )
    mine = lax.dynamic_slice_in_dim(
        owner.reshape(experts, capacity), rank * half_cap, half_cap, axis=1
    ).reshape(-1)
    mine_pair = jnp.maximum(mine, 0)
    mine_rows = jnp.take(dout_f, mine_pair // top, axis=0) * jnp.take(combine, mine_pair)[:, None]
    grad_slots = jnp.where((mine >= 0)[:, None], mine_rows, 0.0).astype(jnp.bfloat16)
    grad_arrived = move_experts(grad_slots.reshape(experts, half_cap, width))
    grad_arrived = lax.all_gather(grad_arrived, "tensor", axis=1, tiled=True)
    grad_blocks = grad_arrived.reshape(groups, local_experts, capacity, width)
    blocks_b, gate_b, up_b, sigma_b, hidden_b = (blocks, gate_act, up_act, sigma, hidden)
    grad_hidden = jnp.einsum(
        "sjcd,jfd->sjcf", grad_blocks, down_weight, preferred_element_type=jnp.float32
    )
    grad_down = jnp.einsum(
        "sjcf,sjcd->jfd", hidden_b, grad_blocks, preferred_element_type=jnp.float32
    )
    grad_gate = (grad_hidden * up_b * sigma_b * (1.0 + gate_b * (1.0 - sigma_b))).astype(
        jnp.bfloat16
    )
    grad_up = (grad_hidden * gate_b * sigma_b).astype(jnp.bfloat16)
    grad_gate_w = jnp.einsum(
        "sjcd,sjcf->jdf", blocks_b, grad_gate, preferred_element_type=jnp.float32
    )
    grad_up_w = jnp.einsum("sjcd,sjcf->jdf", blocks_b, grad_up, preferred_element_type=jnp.float32)
    grad_rows = jnp.einsum(
        "sjcf,jdf->sjcd", grad_gate, gate_weight, preferred_element_type=jnp.float32
    ) + jnp.einsum("sjcf,jdf->sjcd", grad_up, up_weight, preferred_element_type=jnp.float32)
    grad_half = lax.psum_scatter(
        grad_rows.reshape(experts, capacity, width).astype(jnp.bfloat16),
        "tensor",
        scatter_dimension=1,
        tiled=True,
    )
    grad_back = move_experts(grad_half)
    own_offset = slots - rank * half_cap
    own_half = (own_offset >= 0) & (own_offset < half_cap)
    back_rows = jnp.take(
        grad_back.reshape(experts * half_cap, width),
        flat_route * half_cap + jnp.clip(own_offset, 0, half_cap - 1),
        axis=0,
    ).astype(jnp.float32)
    back_rows = jnp.where(own_half[:, None], back_rows, 0.0).reshape(length, top, width)
    onehot_routes = (routes[:, :, None] == jnp.arange(experts)[None, None, :]).astype(jnp.float32)
    grad_prob = jnp.sum(grad_combine[:, :, None] * onehot_routes, axis=1)
    grad_logit = probs * (grad_prob - jnp.sum(probs * grad_prob, axis=-1, keepdims=True))
    router_f = router_weight.astype(jnp.float32)
    grad_two_part = jnp.sum(back_rows, axis=1) + jnp.dot(
        grad_logit, router_f.T, precision=lax.Precision.HIGHEST
    )
    grad_router = jnp.dot(
        normed_two.astype(jnp.float32).T, grad_logit, precision=lax.Precision.HIGHEST
    )
    grad_two = sum_rows(grad_two_part)
    grad_ffgain = jnp.sum(grad_two * resid * scale_two, axis=0)
    grad_resid = grad_out.astype(jnp.float32) + norm_backward(grad_two, resid, scale_two, ff_gf)
    weights_back = (
        lax.all_gather(query_weight, "dp", axis=0, tiled=True),
        lax.all_gather(key_weight, "dp", axis=0, tiled=True),
        lax.all_gather(value_weight, "dp", axis=0, tiled=True),
        lax.all_gather(output_weight, "dp", axis=1, tiled=True),
    )
    query_back, key_back, value_back, output_back = weights_back
    grad_attn = gather_rows(grad_resid.astype(jnp.bfloat16))
    grad_out_w = matmul_left_t(context, grad_attn)
    grad_context = (
        matmul_right_t(grad_attn, output_back).astype(jnp.bfloat16).reshape(length, heads_local, HD)
    )
    attn_prob = jnp.exp(score_block(query_rot, key_rot) - log_total)
    grad_value_f = jnp.einsum(
        "hqk,qhd->khd",
        attn_prob.astype(jnp.bfloat16),
        grad_context,
        preferred_element_type=jnp.float32,
    )
    grad_prob_att = jnp.einsum(
        "qhd,khd->hqk", grad_context, value_heads, preferred_element_type=jnp.float32
    )
    delta = jnp.sum(attn_prob * grad_prob_att, axis=-1, keepdims=True)
    grad_scores = (attn_prob * (grad_prob_att - delta) * inv_root).astype(jnp.bfloat16)
    grad_query_rot = jnp.einsum(
        "hqk,khd->qhd", grad_scores, key_rot, preferred_element_type=jnp.float32
    )
    grad_key_rot = jnp.einsum(
        "hqk,qhd->khd", grad_scores, query_rot, preferred_element_type=jnp.float32
    )
    grad_query_norm = (grad_query_rot * cosine - rotate_half(grad_query_rot * sine)).reshape(
        length, qd_local
    )
    grad_key_norm = (grad_key_rot * cosine - rotate_half(grad_key_rot * sine)).reshape(
        length, qd_local
    )
    grad_qgain = jnp.sum(grad_query_norm * query_proj * query_scale, axis=0)
    grad_kgain = jnp.sum(grad_key_norm * key_proj * key_scale, axis=0)
    upstream_query = grad_query_norm * query_gloc
    upstream_key = grad_key_norm * key_gloc
    query_dot, key_dot = feature_totals(
        jnp.sum(upstream_query * query_proj, axis=-1, keepdims=True),
        jnp.sum(upstream_key * key_proj, axis=-1, keepdims=True),
    )
    grad_query = (
        query_scale * upstream_query
        - query_proj * query_scale * query_scale * query_scale * (query_dot / qd_total)
    ).astype(jnp.bfloat16)
    grad_key = (
        key_scale * upstream_key
        - key_proj * key_scale * key_scale * key_scale * (key_dot / qd_total)
    ).astype(jnp.bfloat16)
    grad_value = grad_value_f.reshape(length, qd_local).astype(jnp.bfloat16)
    grad_query_w = matmul_left_t(normed_one, grad_query)
    grad_key_w = matmul_left_t(normed_one, grad_key)
    grad_value_w = matmul_left_t(normed_one, grad_value)
    grad_one_part = (
        matmul_right_t(grad_query, query_back)
        + matmul_right_t(grad_key, key_back)
        + matmul_right_t(grad_value, value_back)
    )
    grad_one = sum_rows(grad_one_part)
    grad_again = jnp.sum(grad_one * tok_f * scale_one, axis=0)
    grad_tokens = (grad_resid + norm_backward(grad_one, tok_f, scale_one, attn_gf)).astype(
        jnp.bfloat16
    )
    query_shard, key_shard, value_shard, output_shard = (
        lax.psum_scatter(grad_query_w, "dp", scatter_dimension=0, tiled=True),
        lax.psum_scatter(grad_key_w, "dp", scatter_dimension=0, tiled=True),
        lax.psum_scatter(grad_value_w, "dp", scatter_dimension=0, tiled=True),
        lax.psum_scatter(grad_out_w, "dp", scatter_dimension=1, tiled=True),
    )
    qgain_full = lax.dynamic_update_slice_in_dim(
        jnp.zeros((qd_total,), jnp.float32), grad_qgain, rank * qd_local, 0
    )
    kgain_full = lax.dynamic_update_slice_in_dim(
        jnp.zeros((qd_total,), jnp.float32), grad_kgain, rank * qd_local, 0
    )
    router_sum, again_sum, ffgain_sum, qgain_sum, kgain_sum = lax.psum(
        (grad_router, grad_again, grad_ffgain, qgain_full, kgain_full), ("dp", "tensor")
    )
    return (
        block_out,
        grad_tokens,
        again_sum,
        query_shard,
        key_shard,
        value_shard,
        qgain_sum,
        kgain_sum,
        output_shard,
        ffgain_sum,
        router_sum,
        grad_gate_w,
        grad_up_w,
        grad_down,
    )


AXES = ("dp", "tensor")
RING = (0, 1, 3, 2)


def pairs_of(move):
    return [(r * 2 + t, move(r, t)) for r in range(16) for t in range(2)]


def next_on_ring(r, t):
    z = RING[(RING.index(r // 4) + 1) % 4]
    return (z * 4 + r % 4) * 2 + t


PAIRS = {
    "x": pairs_of(lambda r, t: (r ^ 1) * 2 + t),
    "y": pairs_of(lambda r, t: (r ^ 2) * 2 + t),
    "t": pairs_of(lambda r, t: r * 2 + 1 - t),
    "a": pairs_of(lambda r, t: (r ^ (2 if t else 1)) * 2 + t),
    "b": pairs_of(lambda r, t: (r ^ (1 if t else 2)) * 2 + t),
    "z1": pairs_of(lambda r, t: (r ^ 4) * 2 + t),
    "z2": pairs_of(lambda r, t: (r ^ 8) * 2 + t),
    "ring": pairs_of(next_on_ring),
}


def swap(values, way):
    return lax.ppermute(values, AXES, PAIRS[way])


def total(values, ways=("t", "a", "b", "z1", "z2")):
    for way in ways:
        values = values + swap(values, way)
    return values


def add_bf(left, right):
    return (left.astype(jnp.float32) + right.astype(jnp.float32)).astype(jnp.bfloat16)


def gather_all(rows):
    steps = [rows]
    for _ in range(3):
        steps.append(swap(steps[-1], "ring"))
    sets = []
    for piece in steps:
        beside = swap(piece, "a")
        two = jnp.stack([piece, beside])
        sets.append(jnp.stack([two, swap(two, "b")], axis=1))
    return sets


def scatter_plane(part, add):
    half = add(part[:, 0], swap(part[:, 1], "b"))
    return add(half[0], swap(half[1], "a"))


def ring_sum(parts, add):
    running = parts[1]
    for k in (2, 3, 0):
        running = add(parts[k], swap(running, "ring"))
    return running


def pick(flag, left, right):
    return jnp.where(flag, left, right)


def attend_kernel(
    q_ref, k_ref, v_ref, qs_ref, ks_ref, qg_ref, kg_ref, cos_ref, sin_ref, ctx_ref, qr_ref, kr_ref
):
    cosine, sine = cos_ref[...], sin_ref[...]
    query = q_ref[...] * qs_ref[...] * qg_ref[...]
    key = k_ref[...] * ks_ref[...] * kg_ref[...]
    query = (query * cosine + pltpu.roll(query, HD // 2, 1) * sine).astype(jnp.bfloat16)
    key = (key * cosine + pltpu.roll(key, HD // 2, 1) * sine).astype(jnp.bfloat16)
    qr_ref[...] = query
    kr_ref[...] = key
    prob = softmax_block(query, key)
    ctx_ref[...] = jnp.dot(
        prob.astype(jnp.bfloat16), v_ref[...], preferred_element_type=jnp.float32
    ).astype(jnp.bfloat16)


def dot_nt(left, right):
    return lax.dot_general(
        left, right, (((1,), (1,)), ((), ())), preferred_element_type=jnp.float32
    )


def dot_tn(left, right):
    return lax.dot_general(
        left, right, (((0,), (0,)), ((), ())), preferred_element_type=jnp.float32
    )


def softmax_block(query, key):
    scores = dot_nt(query, key) * (1.0 / math.sqrt(HD))
    row = lax.broadcasted_iota(jnp.int32, scores.shape, 0)
    column = lax.broadcasted_iota(jnp.int32, scores.shape, 1)
    scores = jnp.where(row >= column, scores, -jnp.inf)
    top = jnp.max(scores, axis=-1, keepdims=True)
    raised = jnp.exp(scores - top)
    return raised / jnp.sum(raised, axis=-1, keepdims=True)


def attend_back_kernel(
    qr_ref, kr_ref, v_ref, gc_ref, cos_ref, sin_ref, gq_ref, gk_ref, gv_ref
):
    cosine, sine = cos_ref[...], sin_ref[...]
    query, key = qr_ref[...], kr_ref[...]
    grad_context = gc_ref[...]
    prob = softmax_block(query, key)
    gv_ref[...] = dot_tn(prob.astype(jnp.bfloat16), grad_context).astype(jnp.bfloat16)
    grad_prob = dot_nt(grad_context, v_ref[...])
    delta = jnp.sum(prob * grad_prob, axis=-1, keepdims=True)
    grad_scores = (prob * (grad_prob - delta) * (1.0 / math.sqrt(HD))).astype(jnp.bfloat16)
    grad_query = jnp.dot(grad_scores, key, preferred_element_type=jnp.float32)
    grad_key = dot_tn(grad_scores, query)
    gq_ref[...] = grad_query * cosine - pltpu.roll(grad_query, HD // 2, 1) * sine
    gk_ref[...] = grad_key * cosine - pltpu.roll(grad_key, HD // 2, 1) * sine


def attention_call(kernel, kinds, outs, sequences, length, heads):
    def whole(s, h):
        return (0, 0)

    specs = {
        "head": pl.BlockSpec((length, HD), lambda s, h: (s, h)),
        "second": pl.BlockSpec((length, HD), lambda s, h: (s, heads + h)),
        "row": pl.BlockSpec((length, 1), lambda s, h: (s, 0)),
        "gain": pl.BlockSpec((1, HD), lambda s, h: (0, h)),
        "table": pl.BlockSpec((length, HD), whole),
    }
    size = sequences * length * heads
    return pl.pallas_call(
        kernel,
        grid=(sequences, heads),
        in_specs=[specs[kind] for kind in kinds],
        out_specs=[specs["head"]] * len(outs),
        out_shape=[
            jax.ShapeDtypeStruct((sequences * length, heads * HD), dtype) for dtype in outs
        ],
        cost_estimate=pl.CostEstimate(
            flops=size * length * HD * 4, bytes_accessed=size * HD * 12, transcendentals=size * length
        ),
    )


def dense(
    tokens,
    routes,
    attention_gain,
    query_weight,
    key_weight,
    value_weight,
    query_gain,
    key_gain,
    output_weight,
    feedforward_gain,
    router_weight,
    gate_weight,
    up_weight,
    down_weight,
    grad_out,
):
    bf = jnp.bfloat16
    f32 = jnp.float32
    chip = lax.axis_index("dp")
    core = lax.axis_index("tensor")
    x, y, z = chip % 2, (chip // 2) % 2, chip // 4
    first_core = core == 0
    spot = jnp.where(z == 2, 3, jnp.where(z == 3, 2, z))
    rows, width = tokens.shape
    length = routes.shape[0]
    experts = router_weight.shape[1]
    qd_local = query_weight.shape[1]
    qd_total = qd_local * 2
    cols = qd_local // 4
    heads = cols // HD
    block = width // 4
    shard = width // 16
    tok_f = tokens.astype(f32)
    attn_gf = attention_gain.astype(f32)
    ff_gf = feedforward_gain.astype(f32)

    def plane_order(values):
        return jnp.concatenate(
            [
                lax.dynamic_slice_in_dim(values, ring_plane(spot - k) * block, block, 1)
                for k in range(4)
            ],
            axis=1,
        )

    def ring_plane(place):
        place = place % 4
        return jnp.where(place == 2, 3, jnp.where(place == 3, 2, place))

    def whole_order(values):
        return jnp.concatenate(
            [
                lax.dynamic_slice_in_dim(values, ((spot - RING.index(p)) % 4) * block, block, 1)
                for p in range(4)
            ],
            axis=1,
        )

    def to_plane(blocks):
        keep = lax.dynamic_index_in_dim(blocks, x, 1, keepdims=False)
        send = lax.dynamic_index_in_dim(blocks, 1 - x, 1, keepdims=False)
        beside = swap(send, "x")
        both = jnp.stack([keep, beside])
        keep = lax.dynamic_index_in_dim(both, y, 1, keepdims=False)
        send = lax.dynamic_index_in_dim(both, 1 - y, 1, keepdims=False)
        above = swap(send, "y")
        four = [[keep[0], keep[1]], [above[0], above[1]]]
        rows_of = [[pick(y == b, four[0][i], four[1][i]) for i in range(2)] for b in range(2)]
        return [[pick(x == a, rows_of[b][0], rows_of[b][1]) for a in range(2)] for b in range(2)]

    def ring_list(first):
        found = [first]
        for _ in range(3):
            found.append(swap(found[-1], "ring"))
        return found

    def four_blocks(weights, axis):
        parts = [
            [
                jnp.concatenate(
                    [lax.slice_in_dim(w, (b * 2 + a) * cols, (b * 2 + a + 1) * cols, axis=axis) for w in weights],
                    axis=axis,
                )
                for a in range(2)
            ]
            for b in range(2)
        ]
        return jnp.stack([jnp.stack(row) for row in parts])

    with jax.named_scope("weights"):
        pieces = to_plane(four_blocks((query_weight, key_weight), 1))
        qk_chunk = jnp.concatenate([pieces[b][a] for b in range(2) for a in range(2)], axis=0)
        pieces = to_plane(four_blocks((value_weight,), 1))
        value_chunk = jnp.concatenate([pieces[b][a] for b in range(2) for a in range(2)], axis=0)
        pieces = to_plane(four_blocks((output_weight,), 0))
        out_chunk = jnp.concatenate([pieces[b][a] for b in range(2) for a in range(2)], axis=1)
        qk_full = jnp.concatenate(ring_list(qk_chunk), axis=0)
        value_full = jnp.concatenate(ring_list(value_chunk), axis=0)
        out_full = jnp.concatenate(ring_list(out_chunk), axis=1)

    def plane_rows(values):
        beside = swap(values, "a")
        two = jnp.stack([values, beside])
        four = jnp.stack([two, swap(two, "b")], axis=1)
        other = jnp.swapaxes(swap(four, "t"), 0, 1)
        return jnp.concatenate(
            [pick(first_core, four, other), pick(first_core, other, four)], axis=2
        )

    def plane_sum(part):
        halves = part.reshape(2, 2, 2, rows, width)
        mine = lax.dynamic_index_in_dim(halves, core, 2, keepdims=False)
        theirs = lax.dynamic_index_in_dim(halves, 1 - core, 2, keepdims=False).astype(bf)
        joined = add_bf(mine, jnp.swapaxes(swap(theirs, "t"), 0, 1))
        return scatter_plane(joined, add_bf)

    with jax.named_scope("norm_one"):
        scale_one = row_scale(tok_f)
        normed_one = plane_order((tok_f * scale_one * attn_gf).astype(bf))
        normed_one = plane_rows(normed_one).reshape(4 * length, width)

    with jax.named_scope("expert_weights"):
        gate_up = jnp.concatenate(
            [gate_weight[0], swap(gate_weight[0], "t"), up_weight[0], swap(up_weight[0], "t")], axis=1
        )
        down = jnp.concatenate([down_weight[0], swap(down_weight[0], "t")], axis=0)
    units = down.shape[0]

    with jax.named_scope("routes"):
        own_routes = lax.dynamic_slice_in_dim(routes, core * rows, rows, 0)
        named = jnp.any(own_routes.T[None, :, :] == jnp.arange(experts)[:, None, None], axis=1)
        named = named.astype(bf)
        named_sets = gather_all(named)

    with jax.named_scope("qkv"):
        qk_proj = matmul(normed_one, qk_full)
        value_proj = matmul(normed_one, value_full).astype(bf)
        squares = (qk_proj * qk_proj).reshape(4 * length, 2, cols)
        squares = jnp.sum(squares, axis=-1).T.reshape(2, 2, 2, length)

        def sums_of_plane(values):
            values = values + jnp.swapaxes(swap(values, "t"), 1, 2)
            values = values + jnp.flip(swap(values, "a"), 1)
            return values + jnp.flip(swap(values, "b"), 2)

        squares = sums_of_plane(squares)
        scales = lax.rsqrt(squares / qd_total + EPS).reshape(2, 4 * length)
        query_scale, key_scale = scales[0][:, None], scales[1][:, None]
        first_col = core * qd_local + (chip % 4) * cols
        query_g = lax.dynamic_slice_in_dim(query_gain, first_col, cols).astype(f32)[None]
        key_g = lax.dynamic_slice_in_dim(key_gain, first_col, cols).astype(f32)[None]
        cosine, sine = rope_tables(length, HD)
        cosine, sine = cosine[:, 0], sine[:, 0]
        sine = jnp.where(jnp.arange(HD)[None] < HD // 2, -sine, sine)

    with jax.named_scope("attend"):
        context, query_rot, key_rot = attention_call(
            attend_kernel,
            ("head", "second", "head", "row", "row", "gain", "gain", "table", "table"),
            (bf, bf, bf),
            4,
            length,
            heads,
        )(qk_proj, qk_proj, value_proj, query_scale, key_scale, query_g, key_g, cosine, sine)

    with jax.named_scope("project_out"):
        mixed = plane_sum(matmul(context, out_full).reshape(2, 2, length, width))
        resid = tok_f + whole_order(mixed).astype(f32)
        scale_two = row_scale(resid)
        normed_two = (resid * scale_two * ff_gf).astype(bf)
        probs = jax.nn.softmax(matmul(normed_two, router_weight), axis=-1)

    with jax.named_scope("gather_grad_out"):
        grad_sets = gather_all(grad_out)
    with jax.named_scope("gather_rows"):
        row_sets = gather_all(normed_two)

    mine = (jnp.arange(experts) == chip).astype(f32)
    back, hidden_sets, unit_sets, share_sets = [None] * 4, [], [], [None] * 4
    with jax.named_scope("experts"):
        for k in range(4):
            row_k = row_sets[k].reshape(4 * rows, width)
            go_k = grad_sets[k].reshape(4 * rows, width)
            routed = lax.dynamic_index_in_dim(named_sets[k], chip, 2, keepdims=False).astype(f32)
            routed = routed.reshape(4 * rows, 1)
            all_probs = jax.nn.softmax(matmul(row_k, router_weight), axis=-1)
            share = jnp.sum(all_probs * mine, axis=-1, keepdims=True) * routed
            pull = matmul_right_t(go_k, down)
            acts = matmul(row_k, gate_up)
            gate, up = acts[:, :units], acts[:, units:]
            sigma = jax.nn.sigmoid(gate)
            silu = gate * sigma
            hidden = silu * up
            hidden_sets.append((hidden * share).astype(bf))
            grad_combine = jnp.sum(hidden * pull, axis=-1, keepdims=True) * routed
            grad_hidden = pull * share
            grad_gate = (grad_hidden * up * sigma * (1.0 + gate * (1.0 - sigma))).astype(bf)
            grad_up = (grad_hidden * silu).astype(bf)
            grad_units = jnp.concatenate([grad_gate, grad_up], axis=1)
            unit_sets.append(grad_units)
            rows_back = matmul_right_t(grad_units, gate_up).astype(bf)
            back[k] = scatter_plane(rows_back.reshape(2, 2, rows, width), add_bf)
            spread = grad_combine.reshape(2, 2, 1, rows) * mine[:, None]
            share_sets[k] = scatter_plane(spread, jnp.add)
        grad_rows = ring_sum(back, add_bf)
        grad_prob = ring_sum(share_sets, jnp.add).T

    with jax.named_scope("expert_grads"):
        all_rows = jnp.concatenate([s.reshape(4 * rows, width) for s in row_sets], axis=0)
        all_go = jnp.concatenate([s.reshape(4 * rows, width) for s in grad_sets], axis=0)
        all_units = jnp.concatenate(unit_sets, axis=0)
        all_hidden = jnp.concatenate(hidden_sets, axis=0)
        unit_w = matmul_left_t(all_rows, all_units)
        down_w = matmul_left_t(all_hidden, all_go)
        half = units // 2
        grad_gate_w = unit_w[:, :half] + swap(unit_w[:, half:units].astype(bf), "t").astype(f32)
        grad_up_w = unit_w[:, units : units + half] + swap(
            unit_w[:, units + half :].astype(bf), "t"
        ).astype(f32)
        grad_down_w = down_w[:half] + swap(down_w[half:].astype(bf), "t").astype(f32)

    with jax.named_scope("router_back"):
        grad_logit = probs * (grad_prob - jnp.sum(probs * grad_prob, axis=-1, keepdims=True))
        router_f = router_weight.astype(f32)
        grad_two = grad_rows.astype(f32) + jnp.dot(
            grad_logit, router_f.T, precision=lax.Precision.HIGHEST
        )
        grad_router = jnp.dot(
            grad_logit.T, normed_two.astype(f32), precision=lax.Precision.HIGHEST
        )
        grad_ffgain = jnp.sum(grad_two * resid * scale_two, axis=0, keepdims=True)
        grad_resid = grad_out.astype(f32) + norm_backward(grad_two, resid, scale_two, ff_gf)
        early = total(jnp.concatenate([grad_router, grad_ffgain], axis=0))

    with jax.named_scope("expert_out"):
        out_sets = [
            scatter_plane(matmul(h, down).astype(bf).reshape(2, 2, rows, width), add_bf)
            for h in hidden_sets
        ]
        block_out = (resid + ring_sum(out_sets, add_bf).astype(f32)).astype(bf)

    with jax.named_scope("attend_back"):
        grad_attn = plane_rows(plane_order(grad_resid.astype(bf))).reshape(4 * length, width)
        grad_context = matmul_right_t(grad_attn, out_full).astype(bf)
        grad_query_norm, grad_key_norm, grad_value = attention_call(
            attend_back_kernel,
            ("head", "head", "head", "head", "table", "table"),
            (f32, f32, bf),
            4,
            length,
            heads,
        )(query_rot, key_rot, value_proj, grad_context, cosine, sine)
        query_proj, key_proj = qk_proj[:, :cols], qk_proj[:, cols:]
        grad_qgain = jnp.sum(grad_query_norm * query_proj * query_scale, axis=0)
        grad_kgain = jnp.sum(grad_key_norm * key_proj * key_scale, axis=0)
        upstream_query = grad_query_norm * query_g
        upstream_key = grad_key_norm * key_g
        dots = jnp.stack(
            [
                jnp.sum(upstream_query * query_proj, axis=-1),
                jnp.sum(upstream_key * key_proj, axis=-1),
            ]
        )
        dots = sums_of_plane(dots.reshape(2, 2, 2, length)).reshape(2, 4 * length)
        query_dot, key_dot = dots[0][:, None], dots[1][:, None]
        grad_query = (
            query_scale * upstream_query
            - query_proj * query_scale * query_scale * query_scale * (query_dot / qd_total)
        ).astype(bf)
        grad_key = (
            key_scale * upstream_key
            - key_proj * key_scale * key_scale * key_scale * (key_dot / qd_total)
        ).astype(bf)

    def block_of(values, k):
        return values[:, k * block : (k + 1) * block]

    with jax.named_scope("weight_grads"):
        out_parts = [matmul_left_t(context, block_of(grad_attn, k)).astype(bf) for k in range(4)]
        out_sum = ring_sum(out_parts, add_bf)
        out_blocks = jnp.stack(
            [
                jnp.stack([out_sum[:, (b * 2 + a) * shard : (b * 2 + a + 1) * shard] for a in range(2)])
                for b in range(2)
            ]
        )
        pieces = to_plane(out_blocks)
        output_shard = jnp.concatenate(
            [pieces[b][a] for b in range(2) for a in range(2)], axis=0
        ).astype(f32)
        grads = jnp.concatenate([grad_query, grad_key, grad_value], axis=1)
        parts = [matmul_left_t(block_of(normed_one, k), grads).astype(bf) for k in range(4)]
        summed = ring_sum(parts, add_bf)
        pieces = to_plane(summed.reshape(2, 2, shard, 3 * cols))
        gathered = [pieces[b][a].astype(f32) for b in range(2) for a in range(2)]
        query_shard, key_shard, value_shard = (
            jnp.concatenate([p[:, i * cols : (i + 1) * cols] for p in gathered], axis=1)
            for i in range(3)
        )

    with jax.named_scope("grad_tokens"):
        grad_one_part = matmul_right_t(grads[:, : 2 * cols], qk_full) + matmul_right_t(
            grad_value, value_full
        )
        grad_one = plane_sum(grad_one_part.reshape(2, 2, length, width))
        grad_one = whole_order(grad_one).astype(f32)
        grad_again = jnp.sum(grad_one * tok_f * scale_one, axis=0)
        grad_tokens = (grad_resid + norm_backward(grad_one, tok_f, scale_one, attn_gf)).astype(bf)
        wide = jnp.zeros((qd_total,), f32)
        late = total(
            jnp.stack(
                [
                    grad_again,
                    lax.dynamic_update_slice_in_dim(wide, grad_qgain, first_col, 0),
                    lax.dynamic_update_slice_in_dim(wide, grad_kgain, first_col, 0),
                ]
            )
        )
    return (
        block_out,
        grad_tokens,
        late[0],
        query_shard,
        key_shard,
        value_shard,
        late[1],
        late[2],
        output_shard,
        early[experts],
        early[:experts].T,
        grad_gate_w[None],
        grad_up_w[None],
        grad_down_w[None],
    )


def solution(mesh):
    small = mesh.shape["dp"] == 16 and mesh.shape["tensor"] == 2
    return jax.shard_map(
        dense if small else by_capacity,
        mesh=mesh,
        in_specs=(
            P(("dp", "tensor"), None),
            P("dp", None),
            P(),
            P("dp", "tensor"),
            P("dp", "tensor"),
            P("dp", "tensor"),
            P(),
            P(),
            P("tensor", "dp"),
            P(),
            P(),
            P("dp", None, "tensor"),
            P("dp", None, "tensor"),
            P("dp", "tensor", None),
            P(("dp", "tensor"), None),
        ),
        out_specs=(
            P(("dp", "tensor"), None),
            P(("dp", "tensor"), None),
            P(),
            P("dp", "tensor"),
            P("dp", "tensor"),
            P("dp", "tensor"),
            P(),
            P(),
            P("tensor", "dp"),
            P(),
            P(),
            P("dp", None, "tensor"),
            P("dp", None, "tensor"),
            P("dp", "tensor", None),
        ),
        check_vma=False,
    )
```
